512 devices in a mesh: wide: 64 (over y, x, core), freq: 8 (over z).
Axes of the slice: x: 4, y: 8, z: 8, core: 2. Of those that a mesh axis runs over, the one named last changes fastest.
Arguments:
- wave: bfloat16 [2, 8, 1024, 1024], P(None, 'freq', 'wide'), may hold values from -6 to 6
- filters: bfloat16 [2, 2, 8, 3, 81], P(None, None, 'freq'), may hold values from -0.6640625 to 0.6640625
- vel_bins: int32 [2, 2, 3, 1024], replicated, may hold values from 0 to 2
- blend_levels: int32 [2, 2, 3, 1024], replicated, may hold values from 1 to 16
- aperture: int32 [2, 64, 64], replicated, may hold values 0 or 1
Outputs:
- image_shallow: float32 [1024, 1024], P('wide', 'freq')
- image_deep: float32 [1024, 1024], P('wide', 'freq')
The draws below stay inside these ranges and needn't reach their ends.
All inputs are finite; a program needn't handle non-finite values.
Results may differ from the reference program's by a relative error of at most 0.017.
Values may be sent and summed in bfloat16 or wider, within the bound.
A program may use at most 64 MiB of HBM per device.

```python
import jax
import jax.numpy as jnp
from jax import lax

SIDE = 32
TAPS = 9
VBINS = 3
BLEND = 3
NSTEP = 2
BLK = 16
FREQS = 8
POS = 1024
NBLK = 64


def set_ends(entries, stream_key, smallest, largest):
    index_at = [jax.random.randint(jax.random.fold_in(stream_key, axis), (), 0, length) for axis, length in enumerate(entries.shape)]
    widest = entries.shape.index(max(entries.shape))
    beside = index_at[:widest] + [(index_at[widest] + 1) % entries.shape[widest]] + index_at[widest + 1:]
    return entries.at[tuple(index_at)].set(smallest).at[tuple(beside)].set(largest)


def shard_levels(key, extent, shards, smallest, largest):
    loudness = 1.0
    for dim, blocks in shards:
        steps = jax.random.uniform(jax.random.fold_in(jax.random.fold_in(key, 6), dim), (blocks,), jnp.float32, smallest / len(shards), largest / len(shards))
        loudness = loudness * jnp.repeat(jnp.exp(steps), extent[dim] // blocks).reshape((-1,) + (1,) * (len(extent) - 1 - dim))
    return loudness


def scatter_about(key, dims, spread, most, pieces=(), held_as=jnp.bfloat16):
    drawn = jax.random.normal(key, dims, jnp.float32) * spread
    if len(pieces) > 0:
        drawn = shard_levels(key, dims, pieces, -0.22, 0.18) * drawn
    return jnp.clip(drawn, min=-most, max=most).astype(held_as)


def setup_inputs(seed: int = 0) -> dict:
    seeds = jax.random.split(jax.random.key(seed), 6)
    return {
        "wave": scatter_about(seeds[0], (2, FREQS, POS, POS), 1.0, 6.0, ((1, 8), (2, 64))),
        "filters": scatter_about(seeds[1], (NSTEP, 2, FREQS, VBINS, TAPS * TAPS), (1.2 / TAPS), 0.6640625, ((2, 8),)),
        "vel_bins": set_ends(jax.random.randint(seeds[2], (NSTEP, 2, BLEND, POS), 0, VBINS), jax.random.fold_in(seeds[2], 1), 0, VBINS - 1).astype(jnp.int32),
        "blend_levels": set_ends(jax.random.randint(seeds[3], (NSTEP, 2, BLEND, POS), 1, 17), jax.random.fold_in(seeds[3], 1), 1, 16).astype(jnp.int32),
        "aperture": set_ends((jax.random.randint(seeds[4], (NSTEP, NBLK, NBLK), 0, 3) < 2).astype(jnp.int32), jax.random.fold_in(seeds[4], 1), 0, 1),
    }


def blend_table(bin_ids, levels):
    weights = levels.astype(jnp.float32)
    onehot = (bin_ids[:, None, :] == jnp.arange(VBINS, dtype=jnp.int32)[None, :, None]).astype(jnp.float32)
    return jnp.sum(onehot * weights[:, None, :], axis=0) / jnp.sum(weights, axis=0)[None, :]


def extrapolate(field, filters_now, table):
    length = SIDE + TAPS - 1
    half_taps = TAPS // 2

    def one_freq(operands):
        real_part, imag_part, filt_real, filt_imag = operands
        batch_rows = real_part.shape[0]
        grid_field = (real_part.astype(jnp.float32) + 1j * imag_part.astype(jnp.float32)).reshape(batch_rows, SIDE, SIDE)
        kernel = (filt_real.astype(jnp.float32) + 1j * filt_imag.astype(jnp.float32)).reshape(VBINS, TAPS, TAPS)[:, ::-1, ::-1]
        spectra = jnp.fft.fft2(grid_field, s=(length, length))
        kernel_spec = jnp.fft.fft2(kernel, s=(length, length))

        def bin_term(velocity):
            full_field = jnp.fft.ifft2(spectra * kernel_spec[velocity][None])
            cropped = full_field[:, half_taps:half_taps + SIDE, half_taps:half_taps + SIDE].reshape(batch_rows, SIDE * SIDE)
            return table[velocity][None, :] * cropped

        running = bin_term(0)
        for velocity in range(1, VBINS):
            running = running + bin_term(velocity)
        return jnp.stack([jnp.real(running), jnp.imag(running)]).astype(jnp.bfloat16)

    result = lax.map(one_freq, (field[0], field[1], filters_now[0], filters_now[1]))
    return jnp.swapaxes(result, 0, 1)


def aperture_field(blocks):
    return jnp.repeat(jnp.repeat(blocks, BLK, axis=0), BLK, axis=1)


def reference(wave, filters, vel_bins, blend_levels, aperture):
    first = extrapolate(wave, filters[0], blend_table(vel_bins[0, 0], blend_levels[0, 0]))
    second = extrapolate(jnp.swapaxes(first, 2, 3), filters[0], blend_table(vel_bins[0, 1], blend_levels[0, 1]))
    keep_mask = aperture_field(aperture[0]).T
    shallow_field = jnp.where(keep_mask[None, None] > 0, second, jnp.zeros_like(second))
    image_shallow = jnp.sum(shallow_field[0].astype(jnp.float32), axis=0)
    third = extrapolate(shallow_field, filters[1], blend_table(vel_bins[1, 1], blend_levels[1, 1]))
    fourth = extrapolate(jnp.swapaxes(third, 2, 3), filters[1], blend_table(vel_bins[1, 0], blend_levels[1, 0]))
    keep_mask = aperture_field(aperture[1])
    deep_field = jnp.where(keep_mask[None, None] > 0, fourth, jnp.zeros_like(fourth))
    image_deep = jnp.sum(deep_field[0].astype(jnp.float32), axis=0)
    return image_shallow, image_deep
```

```python
import functools

import jax
import jax.numpy as jnp
from jax import lax
from jax.experimental import pallas as pl
from jax.experimental.pallas import tpu as pltpu
from jax.sharding import PartitionSpec as P

SIDE = 32
TAPS = 9
VBINS = 3
BLK = 16
LANES = 128
WIN = 3 * LANES
HALF = TAPS // 2
MESH = pl.DeviceIdType.MESH
F32 = jnp.float32
BF16 = jnp.bfloat16


def iota(shape, dim):
    return lax.broadcasted_iota(jnp.int32, shape, dim)


def one_hot(rows, cols, target):
    return jnp.where(iota((rows, cols), 0) == target, 1.0, 0.0).astype(BF16)


def kernel(
    nt, wave_h, filt_h, bins_h, lev_h, ap_h, shal_o, deep_o,
    wave_v, filt_v, bins_v, lev_v, ap_v, taps_v, band_n, band_t, tab_r, tab_c, mask_s, mask_d,
    send1, ubuf, vbuf, send4, rbuf, dsend, drecv, ssend, srecv,
    in_sem, s1, r1, hs, hr, gs, gr, s4, r4, s5, r5, s6, r6, hub_sem,
):
    sb = LANES // nt
    w = lax.axis_index("wide")
    z = lax.axis_index("freq")
    y = w // nt
    xc = w % nt
    last = nt - 1

    def dev(yy, cc, zz):
        return (yy * nt + cc, zz)

    def remote(src, dst, ssem, rsem, to):
        return pltpu.make_async_remote_copy(
            src_ref=src, dst_ref=dst, send_sem=ssem, recv_sem=rsem, device_id=to, device_id_type=MESH
        )

    barrier = pltpu.get_barrier_semaphore()
    for k in range(1, nt):
        for to in (dev(y, (xc + k) % nt, z), dev((y + k) % nt, xc, z), dev(y, xc, (z + k) % nt)):
            pl.semaphore_signal(barrier, inc=1, device_id=to, device_id_type=MESH)

    loads = [
        pltpu.make_async_copy(h, v, in_sem.at[i])
        for i, (h, v) in enumerate(
            ((filt_h, filt_v), (wave_h, wave_v), (bins_h, bins_v), (lev_h, lev_v), (ap_h, ap_v))
        )
    ]
    for load in loads:
        load.start()

    taps_v[...] = jnp.zeros_like(taps_v)
    near = jnp.abs(iota((SIDE, LANES), 1) % SIDE - iota((SIDE, LANES), 0)) <= HALF
    loads[0].wait()
    for t in range(2):
        for k in range(VBINS):
            taps_v[pl.ds(2 * (VBINS * t + k), 2), pl.ds(0, TAPS * TAPS)] = filt_v[t, k].astype(F32)
    taps = taps_v[...].astype(BF16)

    def spread(rows, col_shift, flip):
        cols = iota((1, 12 * LANES), 1)
        group, m = cols // LANES, (cols + HALF) % LANES
        step, off = m // SIDE, m % SIDE
        a, b = (group - step, 2 * HALF - off) if flip else (4 * (group % 3) + step - group // 3, off)
        good = (a >= 0) & (a < TAPS) & (b >= 0) & (b < TAPS)
        target = jnp.where(good, a * TAPS + b, -1)
        return jnp.dot(taps, one_hot(LANES, 12 * LANES, target), preferred_element_type=F32)

    def banded(row):
        wide = jnp.broadcast_to(row, (SIDE, LANES))
        rolled = pltpu.roll(wide, 0, 1, stride=1, stride_axis=0)
        return jnp.where(near, rolled, 0.0).astype(BF16)

    def build_n(t, rows):
        for part in range(2):
            for k in range(VBINS):
                r = 2 * (VBINS * t + k) + part
                for i in range(12):
                    band_n[t, k, pl.ds(SIDE * i, SIDE), pl.ds(LANES * part, LANES)] = banded(
                        rows[r : r + 1, LANES * i : LANES * (i + 1)]
                    )

    def build_t(t, rows):
        for part in range(2):
            for k in range(VBINS):
                r = 2 * (VBINS * t + k) + part
                for j in range(4):
                    for q in range(3):
                        g = 3 * j + q
                        band_t[t, k, pl.ds(LANES * part + SIDE * j, SIDE), pl.ds(LANES * q, LANES)] = banded(
                            rows[r : r + 1, LANES * g : LANES * (g + 1)]
                        )

    def table(t, q, cols):
        bin_ids = [bins_v[t, j, pl.ds(q, 1), cols] for j in range(VBINS)]
        levels = [lev_v[t, j, pl.ds(q, 1), cols].astype(F32) for j in range(VBINS)]
        total = levels[0] + levels[1] + levels[2]
        rows = []
        for k in range(VBINS):
            hits = [jnp.where(b == k, v, 0.0) for b, v in zip(bin_ids, levels)]
            rows.append((hits[0] + hits[1] + hits[2]) / total)
        return rows

    def table_rows(t):
        for k, row in enumerate(table(t, 0, slice(None))):
            tab_r[t, pl.ds(k, 1), :] = row

    def table_cols(t):
        here = pl.ds(pl.multiple_of(y * LANES, LANES), LANES)
        for k, row in enumerate(table(t, 1, here)):
            tab_c[t, k] = jnp.transpose(jnp.broadcast_to(row, (LANES, LANES)))

    def over_r(field, t, parts):
        zero = jnp.zeros((sb, LANES), BF16)
        rows = []
        for c in range(2):
            for n in range(nt):
                rows.append(
                    jnp.concatenate(
                        [field(c, m) if 0 <= m < nt else zero for m in (n - 1, n, n + 1)], axis=1
                    )
                )
        lhs = jnp.concatenate(rows, axis=0)
        out = [[None] * nt for _ in range(parts)]
        for k in range(VBINS):
            prod = jnp.dot(lhs, band_n[t, k], preferred_element_type=F32)
            for n in range(nt):
                weight = tab_r[t, pl.ds(k, 1), pl.ds(LANES * n, LANES)]
                top = slice(sb * n, sb * (n + 1))
                low = slice(sb * (nt + n), sb * (nt + n + 1))
                terms = [prod[top, :LANES] - prod[low, LANES:]]
                if parts == 2:
                    terms.append(prod[top, LANES:] + prod[low, :LANES])
                for c, term in enumerate(terms):
                    term = weight * term
                    out[c][n] = term if k == 0 else out[c][n] + term
        return out

    def over_s(buf, t):
        rhs = jnp.concatenate(
            [
                jnp.concatenate([buf[q, :, c].reshape(LANES, LANES) for q in range(3)], axis=0)
                for c in range(2)
            ],
            axis=1,
        )
        real = imag = None
        for k in range(VBINS):
            prod = jnp.dot(band_t[t, k], rhs, preferred_element_type=F32)
            weight = tab_c[t, k]
            re = weight * (prod[:LANES, :LANES] - prod[LANES:, LANES:])
            im = weight * (prod[:LANES, LANES:] + prod[LANES:, :LANES])
            real = re if k == 0 else real + re
            imag = im if k == 0 else imag + im
        return real.astype(BF16), imag.astype(BF16)

    rows_n = spread(taps, None, True)
    build_n(0, rows_n)
    loads[2].wait()
    loads[3].wait()
    table_rows(0)
    loads[1].wait()
    first = over_r(lambda c, n: wave_v[c, :, pl.ds(LANES * n, LANES)], 0, 2)
    for c in range(2):
        for n in range(nt):
            send1[n, c] = first[c][n].astype(BF16)
    ubuf[1, xc] = send1[xc]

    @pl.when(y == 0)
    def _():
        ubuf[0] = jnp.zeros_like(ubuf[0])
        vbuf[0] = jnp.zeros_like(vbuf[0])

    @pl.when(y == last)
    def _():
        ubuf[2] = jnp.zeros_like(ubuf[2])
        vbuf[2] = jnp.zeros_like(vbuf[2])

    pl.semaphore_wait(barrier, 3 * (nt - 1))

    out1 = []
    for k in range(1, nt):
        to = (xc + k) % nt
        copy = remote(send1.at[to], ubuf.at[1, xc], s1.at[k - 1], r1.at[xc], dev(y, to, z))
        copy.start()
        out1.append(copy)

    def halo(piece, d):
        return remote(
            ubuf.at[1, piece], ubuf.at[2 - 2 * d, piece], hs.at[d, piece], hr.at[d, piece],
            dev((y + last + 2 * d) % nt, xc, z),
        )

    def pass_on(piece):
        @pl.when(y > 0)
        def _():
            halo(piece, 0).start()

        @pl.when(y < last)
        def _():
            halo(piece, 1).start()

    pass_on(xc)
    rows_t = spread(taps, None, False)
    build_t(0, rows_t)
    table_cols(0)
    loads[4].wait()
    row_pick = jnp.where(
        iota((LANES, nt * LANES // BLK), 1) == iota((LANES, nt * LANES // BLK), 0) // BLK + (LANES // BLK) * y, 1.0, 0.0
    ).astype(BF16)
    col_pick = one_hot(
        nt * LANES // BLK, LANES, iota((nt * LANES // BLK, LANES), 1) // BLK + (LANES // BLK) * xc
    )
    picked = jnp.dot(row_pick, ap_v[0].astype(BF16), preferred_element_type=F32).astype(BF16)
    mask_s[...] = jnp.dot(picked, col_pick, preferred_element_type=F32)

    for k in range(1, nt):
        piece = (xc + k) % nt
        remote(send1.at[piece], ubuf.at[1, piece], s1.at[k - 1], r1.at[piece], dev(y, piece, z)).wait_recv()
        pass_on(piece)

    @pl.when(y == z)
    def _():
        for k in range(1, nt):
            pl.semaphore_signal(hub_sem, inc=1, device_id=dev(y, xc, (z + k) % nt), device_id_type=MESH)

    @pl.when(y > 0)
    def _():
        for piece in range(nt):
            halo(piece, 1).wait_recv()

    @pl.when(y < last)
    def _():
        for piece in range(nt):
            halo(piece, 0).wait_recv()

    second = over_s(ubuf, 0)
    keep = mask_s[...] > 0.5
    for c in range(2):
        vbuf[1, :, c] = jnp.where(keep, second[c], jnp.zeros_like(second[c])).reshape(nt, sb, LANES)

    def halo3(d):
        return remote(
            vbuf.at[1], vbuf.at[2 - 2 * d], gs.at[d], gr.at[d], dev((y + last + 2 * d) % nt, xc, z)
        )

    @pl.when(y > 0)
    def _():
        halo3(0).start()

    @pl.when(y < last)
    def _():
        halo3(1).start()

    build_t(1, rows_t)
    table_cols(1)
    real = jnp.where(keep, second[0], jnp.zeros_like(second[0])).astype(F32)
    ssend[...] = jnp.transpose(real).astype(BF16).reshape(nt, sb, LANES)

    @pl.when(y != z)
    def _():
        pl.semaphore_wait(hub_sem, 1)

    def shallow(rho):
        return remote(ssend.at[rho], srecv.at[z], s6.at[rho], r6.at[z], dev(xc, rho, y))

    def shallow_here(rho):
        return pltpu.make_async_copy(ssend.at[rho], srecv.at[z], r6.at[z])

    for rho in range(nt):
        mine = (z == y) & (xc == y) & (xc == rho)

        @pl.when(mine)
        def _():
            shallow_here(rho).start()

        @pl.when(jnp.logical_not(mine))
        def _():
            shallow(rho).start()

    @pl.when(y > 0)
    def _():
        halo3(1).wait_recv()

    @pl.when(y < last)
    def _():
        halo3(0).wait_recv()

    third = over_s(vbuf, 1)
    for c in range(2):
        send4[:, c] = third[c].reshape(nt, sb, LANES)
    out4 = []
    for k in range(1, nt):
        to = (xc + k) % nt
        copy = remote(send4.at[to], rbuf.at[xc], s4.at[k - 1], r4.at[xc], dev(y, to, z))
        copy.start()
        out4.append(copy)
    rbuf[xc] = send4[xc]
    build_n(1, rows_n)
    table_rows(1)
    blocks = nt * LANES // BLK
    row_pick = jnp.where(
        iota((sb, blocks), 1) == iota((sb, blocks), 0) // BLK + (sb // BLK) * w, 1.0, 0.0
    ).astype(BF16)
    picked = jnp.dot(row_pick, ap_v[1].astype(BF16), preferred_element_type=F32).astype(BF16)
    mask_d[...] = jnp.dot(
        picked, one_hot(blocks, nt * LANES, iota((blocks, nt * LANES), 1) // BLK), preferred_element_type=F32
    )
    for k in range(1, nt):
        piece = (xc + k) % nt
        remote(send4.at[piece], rbuf.at[piece], s4.at[k - 1], r4.at[piece], dev(y, piece, z)).wait_recv()

    fourth = over_r(lambda c, n: rbuf[n, c], 1, 1)[0]
    for n in range(nt):
        keep_n = mask_d[:, pl.ds(LANES * n, LANES)] > 0.5
        tile = fourth[n].astype(BF16)
        dsend[n] = jnp.where(keep_n, tile, jnp.zeros_like(tile))
    out5 = []
    for k in range(1, nt):
        to = (z + k) % nt
        copy = remote(dsend.at[to], drecv.at[z], s5.at[k - 1], r5.at[z], dev(y, xc, to))
        copy.start()
        out5.append(copy)
    drecv[z] = dsend[z]

    for copy in out1 + out4:
        copy.wait_send()

    @pl.when(y > 0)
    def _():
        for piece in range(nt):
            halo(piece, 0).wait_send()
        halo3(0).wait_send()

    @pl.when(y < last)
    def _():
        for piece in range(nt):
            halo(piece, 1).wait_send()
        halo3(1).wait_send()

    for rho in range(nt):
        mine = (z == y) & (xc == y) & (xc == rho)

        @pl.when(jnp.logical_not(mine))
        def _():
            shallow(rho).wait_send()

    for f in range(nt):
        pltpu.make_async_copy(ssend.at[0], srecv.at[f], r6.at[f]).wait()
    shal_o[...] = jnp.sum(srecv[...].astype(F32), axis=0)

    for k in range(1, nt):
        f = (z + k) % nt
        remote(dsend.at[f], drecv.at[f], s5.at[k - 1], r5.at[f], dev(y, xc, f)).wait_recv()
    deep_o[...] = jnp.sum(drecv[...].astype(F32), axis=0)
    for copy in out5:
        copy.wait_send()


def solution(mesh):
    nt = mesh.shape["freq"]
    assert mesh.shape["wide"] == nt * nt
    sb = LANES // nt
    pos = nt * LANES

    def body(wave, filters, vel_bins, blend_levels, aperture):
        wave = wave.reshape(2, sb, pos)
        filters = jnp.transpose(filters, (0, 2, 3, 1, 4)).reshape(2, VBINS, 2, TAPS * TAPS)
        vel_bins = jnp.swapaxes(vel_bins, 1, 2)
        blend_levels = jnp.swapaxes(blend_levels, 1, 2)
        dma = pltpu.SemaphoreType.DMA
        return pl.pallas_call(
            functools.partial(kernel, nt),
            out_shape=(jax.ShapeDtypeStruct((sb, LANES), F32),) * 2,
            in_specs=[pl.BlockSpec(memory_space=pl.ANY)] * 5,
            out_specs=(pl.BlockSpec(memory_space=pltpu.VMEM),) * 2,
            scratch_shapes=[
                pltpu.VMEM(wave.shape, BF16),
                pltpu.VMEM(filters.shape, BF16),
                pltpu.VMEM(vel_bins.shape, jnp.int32),
                pltpu.VMEM(blend_levels.shape, jnp.int32),
                pltpu.VMEM(aperture.shape, jnp.int32),
                pltpu.VMEM((16, LANES), F32),
                pltpu.VMEM((2, VBINS, WIN, 2 * LANES), BF16),
                pltpu.VMEM((2, VBINS, 2 * LANES, WIN), BF16),
                pltpu.VMEM((2, 8, pos), F32),
                pltpu.VMEM((2, VBINS, LANES, LANES), F32),
                pltpu.VMEM((LANES, LANES), F32),
                pltpu.VMEM((sb, pos), F32),
                pltpu.VMEM((nt, 2, sb, LANES), BF16),
                pltpu.VMEM((3, nt, 2, sb, LANES), BF16),
                pltpu.VMEM((3, nt, 2, sb, LANES), BF16),
                pltpu.VMEM((nt, 2, sb, LANES), BF16),
                pltpu.VMEM((nt, 2, sb, LANES), BF16),
                pltpu.VMEM((nt, sb, LANES), BF16),
                pltpu.VMEM((nt, sb, LANES), BF16),
                pltpu.VMEM((nt, sb, LANES), BF16),
                pltpu.VMEM((nt, sb, LANES), BF16),
                dma((5,)),
                dma((nt,)),
                dma((nt,)),
                dma((2, nt)),
                dma((2, nt)),
                dma((2,)),
                dma((2,)),
                dma((nt,)),
                dma((nt,)),
                dma((nt,)),
                dma((nt,)),
                dma((nt,)),
                dma((nt,)),
                pltpu.SemaphoreType.REGULAR,
            ],
            compiler_params=pltpu.CompilerParams(collective_id=0, has_side_effects=True),
            name="sink",
        )(wave, filters, vel_bins, blend_levels, aperture)

    return jax.shard_map(
        body,
        mesh=mesh,
        in_specs=(P(None, "freq", "wide", None), P(None, None, "freq", None, None), P(), P(), P()),
        out_specs=(P("wide", "freq"), P("wide", "freq")),
        check_vma=False,
    )
```

```python
import functools

import jax
import jax.numpy as jnp
from jax import lax
from jax.experimental import pallas as pl
from jax.experimental.pallas import tpu as pltpu
from jax.sharding import PartitionSpec as P

SIDE = 32
TAPS = 9
VBINS = 3
BLK = 16
LANES = 128
WIN = 3 * LANES
HALF = TAPS // 2
MESH = pl.DeviceIdType.MESH
F32 = jnp.float32
BF16 = jnp.bfloat16


def iota(shape, dim):
    return lax.broadcasted_iota(jnp.int32, shape, dim)


def one_hot(rows, cols, target):
    return jnp.where(iota((rows, cols), 0) == target, 1.0, 0.0).astype(BF16)


def kernel(
    nt, wave_h, filt_h, bins_h, lev_h, ap_h, shal_o, deep_o,
    wave_v, filt_v, bins_v, lev_v, ap_v, taps_v, band_n, blend_2, blend_3, tab_r, mask_s, mask_d,
    send1, ubuf, send2, rbuf, dsend, drecv, ssend, srecv,
    in_sem, s1, r1, s2, r2, s5, r5, s6, r6, met1, met2, met3,
):
    sb = LANES // nt
    nx = nt // 2
    w = lax.axis_index("wide")
    z = lax.axis_index("freq")
    y = w // nt
    xc = w % nt
    last = nt - 1

    def dev(yy, cc, zz):
        return (yy * nt + cc, zz)

    def remote(src, dst, ssem, rsem, to):
        return pltpu.make_async_remote_copy(
            src_ref=src, dst_ref=dst, send_sem=ssem, recv_sem=rsem, device_id=to, device_id_type=MESH
        )

    def signal(sem, to):
        pl.semaphore_signal(sem, inc=1, device_id=to, device_id_type=MESH)

    steps = sorted(((i, j) for i in range(nx) for j in range(2)), key=lambda s: (-min(s[0], nx - s[0]), -s[1]))

    def column(i, j):
        return (xc // 2 + i) % nx * 2 + (xc % 2 + j) % 2

    others = [column(i, j) for i, j in steps if (i, j) != (0, 0)]
    beside = sorted({1, last})
    two_off = sorted({2 % nt, (nt - 2) % nt} - {0})

    barrier = pltpu.get_barrier_semaphore()
    for k in beside:
        signal(barrier, dev(y, xc, (z + k) % nt))
        for c in others + [xc]:
            signal(barrier, dev((y + k) % nt, c, z))
    for c in others:
        signal(barrier, dev(y, c, z))

    loads = [
        pltpu.make_async_copy(h, v, in_sem.at[i])
        for i, (h, v) in enumerate(
            ((filt_h, filt_v), (wave_h, wave_v), (bins_h, bins_v), (lev_h, lev_v), (ap_h, ap_v))
        )
    ]
    for load in loads:
        load.start()

    taps_v[...] = jnp.zeros_like(taps_v)
    near = jnp.abs(iota((SIDE, LANES), 1) % SIDE - iota((SIDE, LANES), 0)) <= HALF

    def pick(flip):
        cols = iota((1, 12 * LANES), 1)
        group, m = cols // LANES, (cols + HALF) % LANES
        step, off = m // SIDE, m % SIDE
        a, b = (group - step, 2 * HALF - off) if flip else (4 * (group % 3) + step - group // 3, off)
        good = (a >= 0) & (a < TAPS) & (b >= 0) & (b < TAPS)
        return one_hot(LANES, 12 * LANES, jnp.where(good, a * TAPS + b, -1))

    pick_n = pick(True)
    loads[0].wait()
    for t in range(2):
        for k in range(VBINS):
            taps_v[pl.ds(2 * (VBINS * t + k), 2), pl.ds(0, TAPS * TAPS)] = filt_v[t, k].astype(F32)
    taps = taps_v[...].astype(BF16)

    def banded(rows, r, g):
        wide = jnp.broadcast_to(rows[r : r + 1, LANES * g : LANES * (g + 1)], (SIDE, LANES))
        return pltpu.roll(wide, 0, 1, stride=1, stride_axis=0)

    def build_n(t, rows):
        for part in range(2):
            for k in range(VBINS):
                r = 2 * (VBINS * t + k) + part
                for i in range(12):
                    band_n[t, k, pl.ds(SIDE * i, SIDE), pl.ds(LANES * part, LANES)] = jnp.where(
                        near, banded(rows, r, i), 0.0
                    ).astype(BF16)

    def blended(t, rows, part, j, q, cols):
        total = None
        for k in range(VBINS):
            term = cols[k][SIDE * j : SIDE * (j + 1)] * banded(rows, 2 * (VBINS * t + k) + part, 3 * j + q)
            total = term if k == 0 else total + term
        return jnp.where(near, total, 0.0).astype(BF16)

    def table(t, q, cols):
        bin_ids = [bins_v[t, j, pl.ds(q, 1), cols] for j in range(VBINS)]
        levels = [lev_v[t, j, pl.ds(q, 1), cols].astype(F32) for j in range(VBINS)]
        total = levels[0] + levels[1] + levels[2]
        rows = []
        for k in range(VBINS):
            hits = [jnp.where(b == k, v, 0.0) for b, v in zip(bin_ids, levels)]
            rows.append((hits[0] + hits[1] + hits[2]) / total)
        return rows

    def table_rows(t):
        for k, row in enumerate(table(t, 0, slice(None))):
            tab_r[t, pl.ds(k, 1), :] = row

    def table_cols(t, tile):
        here = pl.ds(pl.multiple_of(tile * LANES, LANES), LANES)
        return [jnp.transpose(jnp.broadcast_to(row, (LANES, LANES))) for row in table(t, 1, here)]

    def over_r(field, t, parts):
        zero = jnp.zeros((sb, LANES), BF16)
        tiles = [[field(c, n) for n in range(nt)] for c in range(2)]
        rows = []
        for c in range(2):
            for n in range(nt):
                rows.append(
                    jnp.concatenate(
                        [tiles[c][m] if 0 <= m < nt else zero for m in (n - 1, n, n + 1)], axis=1
                    )
                )
        lhs = jnp.concatenate(rows, axis=0)
        out = [[None] * nt for _ in range(parts)]
        for k in range(VBINS):
            prod = jnp.dot(lhs, band_n[t, k], preferred_element_type=F32)
            for n in range(nt):
                weight = tab_r[t, pl.ds(k, 1), pl.ds(LANES * n, LANES)]
                top = slice(sb * n, sb * (n + 1))
                low = slice(sb * (nt + n), sb * (nt + n + 1))
                terms = [prod[top, :LANES] - prod[low, LANES:]]
                if parts == 2:
                    terms.append(prod[top, LANES:] + prod[low, :LANES])
                for c, term in enumerate(terms):
                    term = weight * term
                    out[c][n] = term if k == 0 else out[c][n] + term
        return out

    def complex_of(prod):
        return (
            (prod[:LANES, :LANES] - prod[LANES:, LANES:]).astype(BF16),
            (prod[:LANES, LANES:] + prod[LANES:, :LANES]).astype(BF16),
        )

    rows_n = jnp.dot(taps, pick_n, preferred_element_type=F32)
    build_n(0, rows_n)
    loads[2].wait()
    loads[3].wait()
    table_rows(0)
    loads[1].wait()
    first = over_r(lambda c, n: wave_v[c, :, pl.ds(LANES * n, LANES)], 0, 2)
    for c in range(2):
        for n in range(nt):
            send1[n, c] = first[c][n].astype(BF16)

    @pl.when(y == 0)
    def _():
        ubuf[0] = jnp.zeros_like(ubuf[0])
        rbuf[0] = jnp.zeros_like(rbuf[0])

    @pl.when(y == last)
    def _():
        ubuf[2] = jnp.zeros_like(ubuf[2])
        rbuf[2] = jnp.zeros_like(rbuf[2])

    pl.semaphore_wait(barrier, len(beside) * (nt + 1) + last)

    def to_row(d, start, copy):
        def run():
            for c in others + ([xc] if d else []):
                if start:
                    copy(1 - d, c).start()
                else:
                    copy(1 - d, c).wait_send()

        if d == 0:
            run()
        else:
            pl.when(y < last if d > 0 else y > 0)(run)

    def arrive(copy):
        def run(q):
            for c in others[::-1] + ([xc] if q != 1 else []):
                copy(q, c).wait_recv()

        run(1)
        pl.when(y > 0)(lambda: run(0))
        pl.when(y < last)(lambda: run(2))

    def there(q, c):
        return dev((y + 1 - q + nt) % nt, c, z)

    def copy1(q, c):
        return remote(send1.at[c], ubuf.at[q, xc], s1.at[q, c], r1.at[q, xc], there(q, c))

    def copy1_in(q, c):
        return remote(send1.at[c], ubuf.at[q, c], s1.at[q, c], r1.at[q, c], there(q, c))

    def copy2(q, c):
        return remote(send2.at[q, c], rbuf.at[q, xc], s2.at[q, c], r2.at[q, xc], there(q, c))

    def copy2_in(q, c):
        return remote(send2.at[q, c], rbuf.at[q, c], s2.at[q, c], r2.at[q, c], there(q, c))

    for d in (1, -1, 0):
        to_row(d, True, copy1)
    for k in beside:
        signal(met1, dev((y + k) % nt, xc, z))
        signal(met1, dev(y, xc, (z + k) % nt))
    ubuf[1, xc] = send1[xc]

    rows_t = jnp.dot(taps, pick(False), preferred_element_type=F32)
    cols = table_cols(0, y)
    for part in range(2):
        for j in range(4):
            for q in range(3):
                blend_2[pl.ds(LANES * part + SIDE * j, SIDE), pl.ds(LANES * q, LANES)] = blended(
                    0, rows_t, part, j, q, cols
                )
    blocks = nt * LANES // BLK
    per_tile = LANES // BLK
    loads[4].wait()
    row_pick = jnp.where(
        iota((LANES, blocks), 1) == iota((LANES, blocks), 0) // BLK + per_tile * y, 1.0, 0.0
    ).astype(BF16)
    col_pick = one_hot(blocks, LANES, iota((blocks, LANES), 1) // BLK + per_tile * xc)
    picked = jnp.dot(row_pick, ap_v[0].astype(BF16), preferred_element_type=F32).astype(BF16)
    mask_s[...] = jnp.dot(picked, col_pick, preferred_element_type=F32)

    pl.semaphore_wait(met1, 2 * len(beside))
    for k in two_off:
        signal(met2, dev((y + k) % nt, xc, z))
        signal(met2, dev(y, xc, (z + k) % nt))

    for q in range(3):
        cols = table_cols(1, (y + 1 - q + nt) % nt)
        for part in range(2):
            for j in range(4):
                blend_3[q, pl.ds(LANES * part + SIDE * j, SIDE), :] = blended(1, rows_t, part, j, q, cols)

    if two_off:
        pl.semaphore_wait(met2, 2 * len(two_off))
    for k in range(1, nt):
        signal(met3, dev(y, xc, (z + k) % nt))

    build_n(1, rows_n)
    table_rows(1)
    row_pick = jnp.where(
        iota((sb, blocks), 1) == iota((sb, blocks), 0) // BLK + (sb // BLK) * w, 1.0, 0.0
    ).astype(BF16)
    picked = jnp.dot(row_pick, ap_v[1].astype(BF16), preferred_element_type=F32).astype(BF16)
    mask_d[...] = jnp.dot(
        picked, one_hot(blocks, nt * LANES, iota((blocks, nt * LANES), 1) // BLK), preferred_element_type=F32
    )

    arrive(copy1_in)

    rhs = jnp.concatenate(
        [
            jnp.concatenate([ubuf[q, :, c].reshape(LANES, LANES) for q in range(3)], axis=0)
            for c in range(2)
        ],
        axis=1,
    )
    keep = mask_s[...] > 0.5
    field = [
        jnp.where(keep, part, jnp.zeros_like(part))
        for part in complex_of(jnp.dot(blend_2[...], rhs, preferred_element_type=F32))
    ]

    rhs = jnp.concatenate(field, axis=1)
    for d in (1, -1, 0):
        q = 1 - d
        for c, part in enumerate(complex_of(jnp.dot(blend_3[q], rhs, preferred_element_type=F32))):
            send2[q, :, c] = part.reshape(nt, sb, LANES)
        to_row(d, True, copy2)
    rbuf[1, xc] = send2[1, xc]

    ssend[...] = jnp.transpose(field[0].astype(F32)).astype(BF16).reshape(nt, sb, LANES)
    pl.semaphore_wait(met3, last)

    def shallow(rho):
        return remote(ssend.at[rho], srecv.at[z], s6.at[rho], r6.at[z], dev(xc, rho, y))

    def shallow_here(rho):
        return pltpu.make_async_copy(ssend.at[rho], srecv.at[z], r6.at[z])

    for rho in range(nt):
        mine = (z == y) & (xc == y) & (xc == rho)

        @pl.when(mine)
        def _():
            shallow_here(rho).start()

        @pl.when(jnp.logical_not(mine))
        def _():
            shallow(rho).start()

    arrive(copy2_in)

    def third(c, n):
        return (rbuf[0, n, c].astype(F32) + rbuf[1, n, c].astype(F32) + rbuf[2, n, c].astype(F32)).astype(BF16)

    fourth = over_r(third, 1, 1)[0]
    for n in range(nt):
        keep_n = mask_d[:, pl.ds(LANES * n, LANES)] > 0.5
        tile = fourth[n].astype(BF16)
        dsend[n] = jnp.where(keep_n, tile, jnp.zeros_like(tile))
    out5 = []
    for k in sorted(range(1, nt), key=lambda k: -min(k, nt - k)):
        to = (z + k) % nt
        copy = remote(dsend.at[to], drecv.at[z], s5.at[k - 1], r5.at[z], dev(y, xc, to))
        copy.start()
        out5.append(copy)
    drecv[z] = dsend[z]

    for d in (1, -1, 0):
        to_row(d, False, copy1)
        to_row(d, False, copy2)
    for rho in range(nt):
        mine = (z == y) & (xc == y) & (xc == rho)

        @pl.when(jnp.logical_not(mine))
        def _():
            shallow(rho).wait_send()

    for f in range(nt):
        pltpu.make_async_copy(ssend.at[0], srecv.at[f], r6.at[f]).wait()
    shal_o[...] = jnp.sum(srecv[...].astype(F32), axis=0)

    for k in range(1, nt):
        f = (z + k) % nt
        remote(dsend.at[f], drecv.at[f], s5.at[k - 1], r5.at[f], dev(y, xc, f)).wait_recv()
    deep_o[...] = jnp.sum(drecv[...].astype(F32), axis=0)
    for copy in out5:
        copy.wait_send()


def solution(mesh):
    nt = mesh.shape["freq"]
    assert mesh.shape["wide"] == nt * nt
    sb = LANES // nt
    pos = nt * LANES

    def body(wave, filters, vel_bins, blend_levels, aperture):
        wave = wave.reshape(2, sb, pos)
        filters = jnp.transpose(filters, (0, 2, 3, 1, 4)).reshape(2, VBINS, 2, TAPS * TAPS)
        vel_bins = jnp.swapaxes(vel_bins, 1, 2)
        blend_levels = jnp.swapaxes(blend_levels, 1, 2)
        dma = pltpu.SemaphoreType.DMA
        return pl.pallas_call(
            functools.partial(kernel, nt),
            out_shape=(jax.ShapeDtypeStruct((sb, LANES), F32),) * 2,
            in_specs=[pl.BlockSpec(memory_space=pl.ANY)] * 5,
            out_specs=(pl.BlockSpec(memory_space=pltpu.VMEM),) * 2,
            scratch_shapes=[
                pltpu.VMEM(wave.shape, BF16),
                pltpu.VMEM(filters.shape, BF16),
                pltpu.VMEM(vel_bins.shape, jnp.int32),
                pltpu.VMEM(blend_levels.shape, jnp.int32),
                pltpu.VMEM(aperture.shape, jnp.int32),
                pltpu.VMEM((16, LANES), F32),
                pltpu.VMEM((2, VBINS, WIN, 2 * LANES), BF16),
                pltpu.VMEM((2 * LANES, WIN), BF16),
                pltpu.VMEM((3, 2 * LANES, LANES), BF16),
                pltpu.VMEM((2, 8, pos), F32),
                pltpu.VMEM((LANES, LANES), F32),
                pltpu.VMEM((sb, pos), F32),
                pltpu.VMEM((nt, 2, sb, LANES), BF16),
                pltpu.VMEM((3, nt, 2, sb, LANES), BF16),
                pltpu.VMEM((3, nt, 2, sb, LANES), BF16),
                pltpu.VMEM((3, nt, 2, sb, LANES), BF16),
                pltpu.VMEM((nt, sb, LANES), BF16),
                pltpu.VMEM((nt, sb, LANES), BF16),
                pltpu.VMEM((nt, sb, LANES), BF16),
                pltpu.VMEM((nt, sb, LANES), BF16),
                dma((5,)),
                dma((3, nt)),
                dma((3, nt)),
                dma((3, nt)),
                dma((3, nt)),
                dma((nt,)),
                dma((nt,)),
                dma((nt,)),
                dma((nt,)),
                pltpu.SemaphoreType.REGULAR,
                pltpu.SemaphoreType.REGULAR,
                pltpu.SemaphoreType.REGULAR,
            ],
            compiler_params=pltpu.CompilerParams(collective_id=0, has_side_effects=True),
            name="sink",
        )(wave, filters, vel_bins, blend_levels, aperture)

    return jax.shard_map(
        body,
        mesh=mesh,
        in_specs=(P(None, "freq", "wide", None), P(None, None, "freq", None, None), P(), P(), P()),
        out_specs=(P("wide", "freq"), P("wide", "freq")),
        check_vma=False,
    )
```

```python
import functools

import jax
import jax.numpy as jnp
from jax import lax
from jax.experimental import pallas as pl
from jax.experimental.pallas import tpu as pltpu
from jax.sharding import PartitionSpec as P

SIDE = 32
TAPS = 9
VBINS = 3
BLK = 16
LANES = 128
WIN = 3 * LANES
HALF = TAPS // 2
MESH = pl.DeviceIdType.MESH
F32 = jnp.float32
BF16 = jnp.bfloat16


def iota(shape, dim):
    return lax.broadcasted_iota(jnp.int32, shape, dim)


def one_hot(rows, cols, target):
    return jnp.where(iota((rows, cols), 0) == target, 1.0, 0.0).astype(BF16)


def kernel(
    nt, wave_h, filt_h, bins_h, lev_h, ap_h, image_o,
    wave_v, filt_v, bins_v, lev_v, ap_v, taps_v, band_1, band_4, blend_2, blend_3, tab_r, mask_s, mask_d,
    send1, ubuf, send2, rbuf, dsend, drecv, ssend, srecv,
    in_sem, s1, r1, s2, r2, s5, r5, s6, r6, met1, met2, met3,
):
    sb = LANES // nt
    nx = nt // 2
    w = lax.axis_index("wide")
    z = lax.axis_index("freq")
    y = w // nt
    xc = w % nt
    last = nt - 1

    def dev(yy, cc, zz):
        return (yy * nt + cc, zz)

    def remote(src, dst, ssem, rsem, to):
        return pltpu.make_async_remote_copy(
            src_ref=src, dst_ref=dst, send_sem=ssem, recv_sem=rsem, device_id=to, device_id_type=MESH
        )

    def signal(sem, to):
        pl.semaphore_signal(sem, inc=1, device_id=to, device_id_type=MESH)

    steps = sorted(((i, j) for i in range(nx) for j in range(2)), key=lambda s: (-min(s[0], nx - s[0]), -s[1]))

    def column(i, j):
        return (xc // 2 + i) % nx * 2 + (xc % 2 + j) % 2

    others = [column(i, j) for i, j in steps if (i, j) != (0, 0)]
    beside = sorted({1, last})
    two_off = sorted({2 % nt, (nt - 2) % nt} - {0})

    loads = [
        pltpu.make_async_copy(h, v, in_sem.at[i])
        for i, (h, v) in enumerate(
            ((filt_h, filt_v), (wave_h, wave_v), (bins_h, bins_v), (lev_h, lev_v), (ap_h, ap_v))
        )
    ]
    for load in loads:
        load.start()

    barrier = pltpu.get_barrier_semaphore()
    for k in beside:
        signal(barrier, dev(y, xc, (z + k) % nt))
        for c in others + [xc]:
            signal(barrier, dev((y + k) % nt, c, z))
    for c in others:
        signal(barrier, dev(y, c, z))

    taps_v[...] = jnp.zeros_like(taps_v)
    near = jnp.abs(iota((SIDE, LANES), 1) % SIDE - iota((SIDE, LANES), 0)) <= HALF

    def pick(flip):
        cols = iota((1, 12 * LANES), 1)
        group, m = cols // LANES, (cols + HALF) % LANES
        step, off = m // SIDE, m % SIDE
        a, b = (group - step, 2 * HALF - off) if flip else (4 * (group % 3) + step - group // 3, off)
        good = (a >= 0) & (a < TAPS) & (b >= 0) & (b < TAPS)
        return one_hot(LANES, 12 * LANES, jnp.where(good, a * TAPS + b, -1))

    pick_n = pick(True)
    loads[0].wait()
    for t in range(2):
        for k in range(VBINS):
            taps_v[pl.ds(2 * (VBINS * t + k), 2), pl.ds(0, TAPS * TAPS)] = filt_v[t, k].astype(F32)
    taps = taps_v[...].astype(BF16)

    def banded(rows, r, g):
        wide = jnp.broadcast_to(rows[r : r + 1, LANES * g : LANES * (g + 1)], (SIDE, LANES))
        return pltpu.roll(wide, 0, 1, stride=1, stride_axis=0)

    def blocks_n(t, rows):
        for part in range(2):
            for k in range(VBINS):
                r = 2 * (VBINS * t + k) + part
                for i in range(12):
                    yield part, k, i, jnp.where(near, banded(rows, r, i), 0.0)

    def blended(t, rows, part, j, q, cols):
        total = None
        for k in range(VBINS):
            term = cols[k][SIDE * j : SIDE * (j + 1)] * banded(rows, 2 * (VBINS * t + k) + part, 3 * j + q)
            total = term if k == 0 else total + term
        return jnp.where(near, total, 0.0).astype(BF16)

    def table(t, q, cols):
        bin_ids = [bins_v[t, j, pl.ds(q, 1), cols] for j in range(VBINS)]
        levels = [lev_v[t, j, pl.ds(q, 1), cols].astype(F32) for j in range(VBINS)]
        total = levels[0] + levels[1] + levels[2]
        rows = []
        for k in range(VBINS):
            hits = [jnp.where(b == k, v, 0.0) for b, v in zip(bin_ids, levels)]
            rows.append((hits[0] + hits[1] + hits[2]) / total)
        return rows

    def table_rows(t):
        for k, row in enumerate(table(t, 0, slice(None))):
            tab_r[t, pl.ds(k, 1), :] = row

    def table_cols(t, tile):
        here = pl.ds(pl.multiple_of(tile * LANES, LANES), LANES)
        return [jnp.transpose(jnp.broadcast_to(row, (LANES, LANES))) for row in table(t, 1, here)]

    def windows(field):
        zero = jnp.zeros((sb, LANES), BF16)
        tiles = [zero] + [field(n) for n in range(nt)] + [zero]
        return jnp.concatenate([jnp.concatenate(tiles[n : n + 3], axis=1) for n in range(nt)], axis=0)

    def weight(t, k, n):
        return tab_r[t, pl.ds(k, 1), pl.ds(LANES * n, LANES)]

    def complex_of(prod):
        return (
            (prod[:LANES, :LANES] - prod[LANES:, LANES:]).astype(BF16),
            (prod[:LANES, LANES:] + prod[LANES:, :LANES]).astype(BF16),
        )

    rows_n = jnp.dot(taps, pick_n, preferred_element_type=F32)
    for part, k, i, block in blocks_n(0, rows_n):
        band_1[k, pl.ds(SIDE * i, SIDE), pl.ds(LANES * part, LANES)] = block.astype(BF16)
    loads[2].wait()
    loads[3].wait()
    table_rows(0)
    loads[1].wait()
    lhs = jnp.concatenate(
        [windows(lambda n: wave_v[c, :, pl.ds(LANES * n, LANES)]) for c in range(2)], axis=0
    )
    first = [[None] * nt for _ in range(2)]
    for k in range(VBINS):
        prod = jnp.dot(lhs, band_1[k], preferred_element_type=F32)
        for n in range(nt):
            top = prod[sb * n : sb * (n + 1)]
            low = prod[sb * (nt + n) : sb * (nt + n + 1)]
            terms = (top[:, :LANES] - low[:, LANES:], top[:, LANES:] + low[:, :LANES])
            for c, term in enumerate(terms):
                term = weight(0, k, n) * term
                first[c][n] = term if k == 0 else first[c][n] + term
    for c in range(2):
        for n in range(nt):
            send1[n, c] = first[c][n].astype(BF16)

    @pl.when(y == 0)
    def _():
        ubuf[0] = jnp.zeros_like(ubuf[0])
        rbuf[0] = jnp.zeros_like(rbuf[0])

    @pl.when(y == last)
    def _():
        ubuf[2] = jnp.zeros_like(ubuf[2])
        rbuf[2] = jnp.zeros_like(rbuf[2])

    pl.semaphore_wait(barrier, len(beside) * (nt + 1) + last)

    def to_row(d, start, copy):
        def run():
            for c in others + ([xc] if d else []):
                if start:
                    copy(1 - d, c).start()
                else:
                    copy(1 - d, c).wait_send()

        if d == 0:
            run()
        else:
            pl.when(y < last if d > 0 else y > 0)(run)

    def arrive(copy):
        def run(q):
            for c in others[::-1] + ([xc] if q != 1 else []):
                copy(q, c).wait_recv()

        run(1)
        pl.when(y > 0)(lambda: run(0))
        pl.when(y < last)(lambda: run(2))

    def there(q, c):
        return dev((y + 1 - q + nt) % nt, c, z)

    def copy1(q, c):
        return remote(send1.at[c], ubuf.at[q, xc], s1.at[q, c], r1.at[q, xc], there(q, c))

    def copy1_in(q, c):
        return remote(send1.at[c], ubuf.at[q, c], s1.at[q, c], r1.at[q, c], there(q, c))

    def copy2(q, c):
        return remote(send2.at[q, c], rbuf.at[q, xc], s2.at[q, c], r2.at[q, xc], there(q, c))

    def copy2_in(q, c):
        return remote(send2.at[q, c], rbuf.at[q, c], s2.at[q, c], r2.at[q, c], there(q, c))

    for d in (1, -1, 0):
        to_row(d, True, copy1)
    for k in beside:
        signal(met1, dev((y + k) % nt, xc, z))
        signal(met1, dev(y, xc, (z + k) % nt))
    ubuf[1, xc] = send1[xc]

    rows_t = jnp.dot(taps, pick(False), preferred_element_type=F32)
    cols = table_cols(0, y)
    for part in range(2):
        for j in range(4):
            for q in range(3):
                blend_2[pl.ds(LANES * part + SIDE * j, SIDE), pl.ds(LANES * q, LANES)] = blended(
                    0, rows_t, part, j, q, cols
                )
    blocks = nt * LANES // BLK
    per_tile = LANES // BLK
    loads[4].wait()
    row_pick = jnp.where(
        iota((LANES, blocks), 1) == iota((LANES, blocks), 0) // BLK + per_tile * y, 1.0, 0.0
    ).astype(BF16)
    col_pick = one_hot(blocks, LANES, iota((blocks, LANES), 1) // BLK + per_tile * xc)
    picked = jnp.dot(row_pick, ap_v[0].astype(BF16), preferred_element_type=F32).astype(BF16)
    mask_s[...] = jnp.dot(picked, col_pick, preferred_element_type=F32)

    pl.semaphore_wait(met1, 2 * len(beside))
    for k in two_off:
        signal(met2, dev((y + k) % nt, xc, z))
        signal(met2, dev(y, xc, (z + k) % nt))

    for q in range(3):
        cols = table_cols(1, (y + 1 - q + nt) % nt)
        for part in range(2):
            for j in range(4):
                blend_3[q, pl.ds(LANES * part + SIDE * j, SIDE), :] = blended(1, rows_t, part, j, q, cols)

    if two_off:
        pl.semaphore_wait(met2, 2 * len(two_off))
    for k in range(1, nt):
        signal(met3, dev(y, xc, (z + k) % nt))

    for part, k, i, block in blocks_n(1, rows_n):
        rows = pl.ds(WIN * part + SIDE * i, SIDE)
        band_4[rows, pl.ds(LANES * k, LANES)] = (block if part == 0 else -block).astype(BF16)
    table_rows(1)
    row_pick = jnp.where(
        iota((sb, blocks), 1) == iota((sb, blocks), 0) // BLK + (sb // BLK) * w, 1.0, 0.0
    ).astype(BF16)
    picked = jnp.dot(row_pick, ap_v[1].astype(BF16), preferred_element_type=F32).astype(BF16)
    mask_d[...] = jnp.dot(
        picked, one_hot(blocks, nt * LANES, iota((blocks, nt * LANES), 1) // BLK), preferred_element_type=F32
    )

    arrive(copy1_in)

    rhs = jnp.concatenate(
        [
            jnp.concatenate([ubuf[q, :, c].reshape(LANES, LANES) for q in range(3)], axis=0)
            for c in range(2)
        ],
        axis=1,
    )
    keep = mask_s[...] > 0.5
    field = [
        jnp.where(keep, part, jnp.zeros_like(part))
        for part in complex_of(jnp.dot(blend_2[...], rhs, preferred_element_type=F32))
    ]

    rhs = jnp.concatenate(field, axis=1)
    for d in (1, -1, 0):
        q = 1 - d
        for c, part in enumerate(complex_of(jnp.dot(blend_3[q], rhs, preferred_element_type=F32))):
            send2[q, :, c] = part.reshape(nt, sb, LANES)
        to_row(d, True, copy2)
    rbuf[1, xc] = send2[1, xc]

    ssend[...] = jnp.transpose(field[0].astype(F32)).astype(BF16).reshape(nt, sb, LANES)
    pl.semaphore_wait(met3, last)

    def shallow(rho):
        return remote(ssend.at[rho], srecv.at[z], s6.at[rho], r6.at[z], dev(xc, rho, y))

    def shallow_here(rho):
        return pltpu.make_async_copy(ssend.at[rho], srecv.at[z], r6.at[z])

    for rho in range(nt):
        mine = (z == y) & (xc == y) & (xc == rho)

        @pl.when(mine)
        def _():
            shallow_here(rho).start()

        @pl.when(jnp.logical_not(mine))
        def _():
            shallow(rho).start()

    arrive(copy2_in)

    def third(c, n):
        return (rbuf[0, n, c].astype(F32) + rbuf[1, n, c].astype(F32) + rbuf[2, n, c].astype(F32)).astype(BF16)

    lhs = jnp.concatenate([windows(functools.partial(third, c)) for c in range(2)], axis=1)
    prod = jnp.dot(lhs, band_4[...], preferred_element_type=F32)
    for n in range(nt):
        rows = prod[sb * n : sb * (n + 1)]
        tile = weight(1, 0, n) * rows[:, :LANES]
        for k in range(1, VBINS):
            tile = tile + weight(1, k, n) * rows[:, LANES * k : LANES * (k + 1)]
        tile = tile.astype(BF16)
        keep_n = mask_d[:, pl.ds(LANES * n, LANES)] > 0.5
        dsend[n] = jnp.where(keep_n, tile, jnp.zeros_like(tile))

    def deep(f):
        return remote(dsend.at[f], drecv.at[z], s5.at[f], r5.at[z], dev(y, xc, f))

    for f in range(nt):
        pl.when(z != f)(deep(f).start)
    drecv[z] = dsend[z]

    for d in (1, -1, 0):
        to_row(d, False, copy1)
        to_row(d, False, copy2)
    for rho in range(nt):
        mine = (z == y) & (xc == y) & (xc == rho)

        @pl.when(jnp.logical_not(mine))
        def _():
            shallow(rho).wait_send()

    for f in range(nt):
        pltpu.make_async_copy(ssend.at[0], srecv.at[f], r6.at[f]).wait()
    image_o[0] = jnp.sum(srecv[...].astype(F32), axis=0)

    for f in range(nt):
        pl.when(z != f)(remote(dsend.at[f], drecv.at[f], s5.at[f], r5.at[f], dev(y, xc, f)).wait_recv)
    image_o[1] = jnp.sum(drecv[...].astype(F32), axis=0)
    for f in range(nt):
        pl.when(z != f)(deep(f).wait_send)


def solution(mesh):
    nt = mesh.shape["freq"]
    assert mesh.shape["wide"] == nt * nt
    sb = LANES // nt
    pos = nt * LANES

    def body(wave, filters, vel_bins, blend_levels, aperture):
        wave = wave.reshape(2, sb, pos)
        filters = jnp.transpose(filters, (0, 2, 3, 1, 4)).reshape(2, VBINS, 2, TAPS * TAPS)
        vel_bins = jnp.swapaxes(vel_bins, 1, 2)
        blend_levels = jnp.swapaxes(blend_levels, 1, 2)
        dma = pltpu.SemaphoreType.DMA
        images = pl.pallas_call(
            functools.partial(kernel, nt),
            out_shape=pltpu.VMEM((2, sb, LANES), F32),
            in_specs=[pl.BlockSpec(memory_space=pl.ANY)] * 5,
            out_specs=pl.BlockSpec(memory_space=pltpu.VMEM),
            scratch_shapes=[
                pltpu.VMEM(wave.shape, BF16),
                pltpu.VMEM(filters.shape, BF16),
                pltpu.VMEM(vel_bins.shape, jnp.int32),
                pltpu.VMEM(blend_levels.shape, jnp.int32),
                pltpu.VMEM(aperture.shape, jnp.int32),
                pltpu.VMEM((16, LANES), F32),
                pltpu.VMEM((VBINS, WIN, 2 * LANES), BF16),
                pltpu.VMEM((2 * WIN, VBINS * LANES), BF16),
                pltpu.VMEM((2 * LANES, WIN), BF16),
                pltpu.VMEM((3, 2 * LANES, LANES), BF16),
                pltpu.VMEM((2, 8, pos), F32),
                pltpu.VMEM((LANES, LANES), F32),
                pltpu.VMEM((sb, pos), F32),
                pltpu.VMEM((nt, 2, sb, LANES), BF16),
                pltpu.VMEM((3, nt, 2, sb, LANES), BF16),
                pltpu.VMEM((3, nt, 2, sb, LANES), BF16),
                pltpu.VMEM((3, nt, 2, sb, LANES), BF16),
                pltpu.VMEM((nt, sb, LANES), BF16),
                pltpu.VMEM((nt, sb, LANES), BF16),
                pltpu.VMEM((nt, sb, LANES), BF16),
                pltpu.VMEM((nt, sb, LANES), BF16),
                dma((5,)),
                dma((3, nt)),
                dma((3, nt)),
                dma((3, nt)),
                dma((3, nt)),
                dma((nt,)),
                dma((nt,)),
                dma((nt,)),
                dma((nt,)),
                pltpu.SemaphoreType.REGULAR,
                pltpu.SemaphoreType.REGULAR,
                pltpu.SemaphoreType.REGULAR,
            ],
            compiler_params=pltpu.CompilerParams(collective_id=0, has_side_effects=True),
            name="sink",
        )(wave, filters, vel_bins, blend_levels, aperture)
        return images[0], images[1]

    return jax.shard_map(
        body,
        mesh=mesh,
        in_specs=(P(None, "freq", "wide", None), P(None, None, "freq", None, None), P(), P(), P()),
        out_specs=(P("wide", "freq"), P("wide", "freq")),
        check_vma=False,
    )
```
